32 devices in a mesh: tm: 8 (over z, y), state: 4 (over x, core).
Axes of the slice: x: 2, y: 2, z: 4, core: 2. Of those that a mesh axis runs over, the one named last changes fastest.
Arguments:
- jacobian: bfloat16 [256, 64, 1024], P('tm', None, 'state'), may hold values from -0.125 to 0.125
- measurement: float32 [256, 64], P('tm'), may hold values from -6 to 6
- depth_block: int32 [256], P('tm'), may hold values from 0 to 4799
- precision: float32 [4800], replicated, may hold values from 0.25 to 4
- valid_slot_counts: int32 [8], P('tm'), may hold values from 10 to 32, as said below
- retention: float32 [40, 1024], P('tm'), may hold values from 0.45 to 1, as said below
Outputs:
- info_diagonal: float32 [8192], P(('tm', 'state'))
- info_vector: float32 [8192], P(('tm', 'state'))
- final_info: float32 [1024, 1024], P('state', 'tm')
The draws below stay inside these ranges and needn't reach their ends.
Inputs may be any that keep to these rules, and one draw needn't show every extreme that they name: `valid_slot_counts`: each frame block has at least 10 and at most 32 valid slots; in every draw some block has exactly 32 and some exactly 10. `retention`: every factor is positive and at most one.
All inputs are finite; a program needn't handle non-finite values.
Results may differ from the reference program's by a relative error of at most 0.0039.
Values may be sent and summed in bfloat16 or wider, within the bound.
A program may use at most 64 MiB of HBM per device.

```python
import math
import jax
import jax.numpy as jnp
from jax import lax

WARP_TERMS = 1024
DEPTH_ROW_COUNT = 64
NB = 4800
BLOCK_SLOT_COUNT = 32
FR_DEV = 5
BLOCKS = 256
IMAGE_TALLY = 40
N_TM = 8


def draw_valid_slot_counts(key, part):
    key_one, key_two, key_three = jax.random.split(key, 3)
    lowest = BLOCK_SLOT_COUNT // 3
    live = jax.random.randint(key_one, (N_TM,), lowest, BLOCK_SLOT_COUNT + 1)
    first_pick = jax.random.randint(key_two, (), 0, N_TM)
    second_pick = (first_pick + 1 + jax.random.randint(key_three, (), 0, N_TM - 1)) % N_TM
    live = live.at[first_pick].set(BLOCK_SLOT_COUNT).at[second_pick].set(lowest)
    return live.astype(jnp.int32)


def draw_retention(key, part):
    generator_seed_divide = jax.random.split(key, 6)
    fast_share = 0.5
    fast_mask = jax.random.uniform(generator_seed_divide[0], (WARP_TERMS,)) < fast_share
    slow_rate = jax.random.uniform(generator_seed_divide[1], (WARP_TERMS,), minval=0.05, maxval=0.6) * (2.3 / IMAGE_TALLY)
    fast_rate = jax.random.uniform(generator_seed_divide[2], (WARP_TERMS,), minval=1.0 / 50.0, maxval=1.0 / 30.0)
    decay_rates = jnp.where(fast_mask, fast_rate, slow_rate)
    stochastic_jitter = jax.random.uniform(generator_seed_divide[3], (IMAGE_TALLY, WARP_TERMS), minval=0.5, maxval=1.5)
    clustered_loss_height = jax.random.uniform(generator_seed_divide[4], (IMAGE_TALLY, 1)) < 4.0 / IMAGE_TALLY
    clustered_loss_mask = jax.random.uniform(generator_seed_divide[5], (IMAGE_TALLY, WARP_TERMS), minval=0.5, maxval=0.8)
    decay_scaling = jnp.exp(-decay_rates[None, :] * stochastic_jitter) * jnp.where(clustered_loss_height, clustered_loss_mask, 1.0)
    return decay_scaling.astype(jnp.float32)


def plant(entries, rng, low, high):
    place = [jax.random.randint(jax.random.fold_in(rng, axis), (), 0, length) for axis, length in enumerate(entries.shape)]
    main_axis = entries.shape.index(max(entries.shape))
    neighbour = place[:main_axis] + [(place[main_axis] + 1) % entries.shape[main_axis]] + place[main_axis + 1:]
    return entries.at[tuple(place)].set(low).at[tuple(neighbour)].set(high)


def block_scale(stream_key, extent, pieces, low, high):
    def one(position, shards_of):
        heights = jax.random.uniform(jax.random.fold_in(jax.random.fold_in(stream_key, 6), position), (shards_of,), jnp.float32, low / len(pieces), high / len(pieces))
        return jnp.repeat(jnp.exp(heights), extent[position] // shards_of).reshape((-1,) + (1,) * (len(extent) - position - 1))

    factor_of = one(*pieces[0])
    for cut in pieces[1:]:
        factor_of = factor_of * one(*cut)
    return factor_of


def noise(stream_key, extent, scale, bound, cuts=(), held_as=jnp.bfloat16):
    result = jax.random.normal(stream_key, extent, jnp.float32) * scale
    if len(cuts) > 0:
        result = block_scale(stream_key, extent, cuts, -0.22, 0.18) * result
    return jnp.clip(result, min=-bound, max=bound).astype(held_as)


def setup_inputs(seed: int = 0) -> dict:
    splits = jax.random.split(jax.random.key(seed), 7)
    return {
        "jacobian": noise(splits[0], (BLOCKS, DEPTH_ROW_COUNT, WARP_TERMS), (DEPTH_ROW_COUNT * BLOCK_SLOT_COUNT) ** -0.5, 0.125, ((0, 8), (2, 4))),
        "measurement": noise(splits[1], (BLOCKS, DEPTH_ROW_COUNT), 1.0, 6.0, ((0, 8),), jnp.float32),
        "depth_block": plant(jax.random.randint(splits[2], (BLOCKS,), 0, NB), jax.random.fold_in(splits[2], 1), 0, NB - 1).astype(jnp.int32),
        "precision": jnp.clip(jnp.exp(jax.random.uniform(splits[3], (NB,), jnp.float32, math.log(0.25), math.log(4.0))), 0.25, 4.0),
        "valid_slot_counts": draw_valid_slot_counts(jax.random.fold_in(splits[6], 71), 0),
        "retention": draw_retention(jax.random.fold_in(splits[6], 71), 0),
    }


def local_tables(block_forget_factor, active_slot_count, depth_row_index, precision, n_slots):
    frame_total = block_forget_factor.shape[0]
    backward = jnp.flip(jnp.cumprod(jnp.flip(block_forget_factor, 0), 0), 0)
    through = backward[0]
    kept = jnp.concatenate([backward[1:], jnp.ones((1, block_forget_factor.shape[1]), block_forget_factor.dtype)], 0)
    slot_ids = jnp.arange(n_slots, dtype=jnp.int32)
    frames = slot_ids * frame_total // active_slot_count
    onehot = (frames[:, None] == jnp.arange(frame_total, dtype=jnp.int32)[None, :]).astype(block_forget_factor.dtype)
    colfac = jnp.dot(onehot, kept, precision=lax.Precision.HIGHEST)
    matches = depth_row_index[:, None] == jnp.arange(precision.shape[0], dtype=jnp.int32)[None, :]
    picked = lax.optimization_barrier(jnp.sum(jnp.where(matches, precision[None, :], 0.0), axis=1))
    row_multiplier = jnp.where(slot_ids < active_slot_count, jnp.sqrt(picked), 0.0)
    return (through, colfac, row_multiplier)

def scale_blocks(block_jacobian_matrix, row_multiplier, colfac):
    scaled = block_jacobian_matrix.astype(jnp.float32) * row_multiplier[:, None, None] * colfac[:, None, :]
    return scaled.astype(jnp.bfloat16).reshape(-1, block_jacobian_matrix.shape[2])

def reference(jacobian, measurement, depth_block, precision, valid_slot_counts, retention):
    jacobian_stack_total = jacobian.reshape(N_TM, BLOCK_SLOT_COUNT, DEPTH_ROW_COUNT, WARP_TERMS)
    observations_total = measurement.reshape(N_TM, BLOCK_SLOT_COUNT, DEPTH_ROW_COUNT)
    depth_readings_total = depth_block.reshape(N_TM, BLOCK_SLOT_COUNT)
    forget_factors_total = retention.reshape(N_TM, FR_DEV, WARP_TERMS)

    def step_forward(state_pair, input_arrays):
        info_rows, info_vec = state_pair
        block_jacobian_matrix, block_observations, depth_row_index, active_slot_count, block_forget_factor = input_arrays
        through, colfac, row_multiplier = local_tables(block_forget_factor, active_slot_count, depth_row_index, precision, BLOCK_SLOT_COUNT)
        scaled = scale_blocks(block_jacobian_matrix, row_multiplier, colfac)
        weighted_jacobian = (block_observations * row_multiplier[:, None]).astype(jnp.bfloat16).reshape(-1)
        gram_full = lax.dot_general(scaled, scaled, (((0,), (0,)), ((), ())), preferred_element_type=jnp.float32)
        own_vector = jnp.dot(weighted_jacobian, scaled, preferred_element_type=jnp.float32)
        info_rows = through[:, None] * info_rows * through[None, :] + gram_full
        info_vec = through * info_vec + own_vector
        return ((info_rows, info_vec), (jnp.diagonal(info_rows), info_vec))
    begin_offset = (jnp.zeros((WARP_TERMS, WARP_TERMS), jnp.float32), jnp.zeros((WARP_TERMS,), jnp.float32))
    last_state, stacked_arrays = lax.scan(step_forward, begin_offset, (jacobian_stack_total, observations_total, depth_readings_total, valid_slot_counts, forget_factors_total))
    return (stacked_arrays[0].reshape(N_TM * WARP_TERMS), stacked_arrays[1].reshape(N_TM * WARP_TERMS), last_state[0])
```

```python
import functools
import jax
import jax.numpy as jnp
from jax import lax
from jax.experimental import pallas as pl
from jax.experimental.pallas import tpu as pltpu
from jax.sharding import PartitionSpec as P


def local_tables(block_forget_factor, active_slot_count, depth_row_index, precision, n_slots):
    frame_total = block_forget_factor.shape[0]
    backward = jnp.flip(jnp.cumprod(jnp.flip(block_forget_factor, 0), 0), 0)
    through = backward[0]
    kept = jnp.concatenate(
        [backward[1:], jnp.ones((1, block_forget_factor.shape[1]), block_forget_factor.dtype)], 0
    )
    slot_ids = jnp.arange(n_slots, dtype=jnp.int32)
    frames = slot_ids * frame_total // active_slot_count
    onehot = (frames[:, None] == jnp.arange(frame_total, dtype=jnp.int32)[None, :]).astype(
        block_forget_factor.dtype
    )
    colfac = jnp.dot(onehot, kept, precision=lax.Precision.HIGHEST)
    matches = depth_row_index[:, None] == jnp.arange(precision.shape[0], dtype=jnp.int32)[None, :]
    picked = jnp.sum(jnp.where(matches, precision[None, :], 0.0), axis=1)
    row_multiplier = jnp.where(slot_ids < active_slot_count, jnp.sqrt(picked), 0.0)
    return (through, colfac, row_multiplier)


def scale_blocks(block_jacobian_matrix, row_multiplier, colfac):
    scaled = (
        block_jacobian_matrix.astype(jnp.float32)
        * row_multiplier[:, None, None]
        * colfac[:, None, :]
    )
    return scaled.astype(jnp.bfloat16).reshape(-1, block_jacobian_matrix.shape[2])


def gram_slab(block_jacobian_matrix, row_multiplier, colfac, row_start, row_count):
    scaled = scale_blocks(block_jacobian_matrix, row_multiplier, colfac)
    left_cols = lax.dynamic_slice_in_dim(scaled, row_start, row_count, 1)
    return lax.dot_general(
        left_cols, scaled, (((0,), (0,)), ((), ())), preferred_element_type=jnp.float32
    )


def local(jacobian, measurement, depth_block, precision, valid_slot_counts, retention):
    n_slots = jacobian.shape[0]
    stripe_width = jacobian.shape[2]
    stripes = lax.axis_size("state")
    stripe = lax.axis_index("state")
    position = lax.axis_index("tm")
    full_width = stripe_width * stripes
    active_slot_count = valid_slot_counts[0]
    through, colfac, row_multiplier = local_tables(
        retention, active_slot_count, depth_block, precision, n_slots
    )
    own_colfac = lax.dynamic_slice_in_dim(colfac, stripe * stripe_width, stripe_width, 1)
    local_scaled = scale_blocks(jacobian, row_multiplier, own_colfac)
    weighted_jacobian = (measurement * row_multiplier[:, None]).astype(jnp.bfloat16).reshape(-1)
    own_vector = jnp.dot(weighted_jacobian, local_scaled, preferred_element_type=jnp.float32)
    whole_jac = lax.all_gather(jacobian, "state", axis=2, tiled=True)
    gram_rows = gram_slab(whole_jac, row_multiplier, colfac, stripe * stripe_width, stripe_width)
    own_block = lax.dynamic_slice_in_dim(gram_rows, stripe * stripe_width, stripe_width, 1)
    own_diagonal = jnp.diagonal(own_block)

    def combine(earlier, later):
        later_rows = lax.dynamic_slice_in_dim(
            later[0], stripe * stripe_width, stripe_width, later[0].ndim - 1
        )
        product = earlier[0] * later[0]
        diag_next = later_rows * later_rows * earlier[1] + later[1]
        vec_next = later_rows * earlier[2] + later[2]
        return (product, diag_next, vec_next)

    all_through, all_diagonal, all_vector = (
        lax.all_gather(through[None, :], "tm", axis=0, tiled=True),
        lax.all_gather(own_diagonal[None, :], "tm", axis=0, tiled=True),
        lax.all_gather(own_vector[None, :], "tm", axis=0, tiled=True),
    )
    running = lax.associative_scan(combine, (all_through, all_diagonal, all_vector), axis=0)
    info_diagonal = lax.dynamic_index_in_dim(running[1], position, 0, keepdims=False)
    info_vector = lax.dynamic_index_in_dim(running[2], position, 0, keepdims=False)
    backward_decay = jnp.flip(jnp.cumprod(jnp.flip(all_through, 0), 0), 0)
    padded_decay = jnp.concatenate([backward_decay, jnp.ones((1, full_width), jnp.float32)], 0)
    later_weight = lax.dynamic_index_in_dim(padded_decay, position + 1, 0, keepdims=False)
    later_stripe = lax.dynamic_slice_in_dim(later_weight, stripe * stripe_width, stripe_width, 0)
    decayed_rows = later_stripe[:, None] * gram_rows * later_weight[None, :]
    final_info = lax.psum_scatter(decayed_rows, "tm", scatter_dimension=1, tiled=True)
    return (info_diagonal, info_vector, final_info)


MESH = pl.DeviceIdType.MESH
LANES = 128
GROUP = 8


def filter_kernel(
    n_tm,
    jac,
    meas,
    depth,
    prec,
    live,
    ret,
    diag_out,
    vec_out,
    info_out,
    partner_jac,
    across_jac,
    relay_jac,
    weight,
    own_t,
    small,
    later,
    row_decay,
    outgoing,
    incoming,
    jac_send,
    jac_recv,
    small_send,
    small_recv,
    gram_send,
    gram_recv,
):
    t = lax.axis_index("tm")
    s = lax.axis_index("state")
    x = s // 2
    c = s % 2
    partner = (t, x * 2 + 1 - c)
    across = (t, (1 - x) * 2 + c)
    n_slots, n_rows, width = jac.shape
    n_frames, full = ret.shape
    stripes = full // width
    groups = n_slots // GROUP
    depth_rows = GROUP * n_rows

    barrier = pltpu.get_barrier_semaphore()
    for device in (partner, across):
        pl.semaphore_signal(barrier, inc=1, device_id=device, device_id_type=MESH)
    for step in range(1, n_tm):
        pl.semaphore_signal(
            barrier, inc=1, device_id=(lax.rem(t + step, n_tm), s), device_id_type=MESH
        )
    pl.semaphore_wait(barrier, n_tm + 1)

    def lanes(half):
        return pl.ds(pl.multiple_of(half * LANES, LANES), LANES)

    def cross_copy(phase):
        half = lax.rem(c + phase, 2)
        return pltpu.make_async_remote_copy(
            src_ref=jac.at[:, :, lanes(half)],
            dst_ref=across_jac.at[phase],
            send_sem=jac_send.at[phase],
            recv_sem=jac_recv.at[phase],
            device_id=across,
            device_id_type=MESH,
        )

    def relay_copy(phase):
        return pltpu.make_async_remote_copy(
            src_ref=across_jac.at[phase],
            dst_ref=relay_jac.at[phase],
            send_sem=jac_send.at[2 + phase],
            recv_sem=jac_recv.at[2 + phase],
            device_id=partner,
            device_id_type=MESH,
        )

    partner_copy = pltpu.make_async_remote_copy(
        src_ref=jac,
        dst_ref=partner_jac,
        send_sem=jac_send.at[4],
        recv_sem=jac_recv.at[4],
        device_id=partner,
        device_id_type=MESH,
    )
    cross_copy(0).start()
    cross_copy(1).start()
    partner_copy.start()

    active = live[0]
    slot_col = lax.broadcasted_iota(jnp.int32, (n_slots, 1), 0)
    eye = lax.broadcasted_iota(jnp.int32, (n_slots, n_slots), 0) == lax.broadcasted_iota(
        jnp.int32, (n_slots, n_slots), 1
    )
    depth_col = jnp.sum(
        jnp.where(eye, jnp.broadcast_to(depth[...], (n_slots, n_slots)), 0), axis=1, keepdims=True
    )
    picks = depth_col == lax.broadcasted_iota(jnp.int32, (n_slots, prec.shape[1]), 1)
    picked = jnp.sum(jnp.where(picks, prec[...], 0.0), axis=1, keepdims=True)
    row_weight = jnp.where(slot_col < active, jnp.sqrt(picked), 0.0)
    factor = ret[pl.ds(n_frames - 1, 1), :]
    colfac = jnp.ones((n_slots, full), jnp.float32)
    for frame in range(n_frames - 2, -1, -1):
        colfac = jnp.where(slot_col * n_frames < (frame + 1) * active, factor, colfac)
        factor = factor * ret[pl.ds(frame, 1), :]
    weight[...] = row_weight * colfac
    measured = (meas[...] * row_weight).astype(jnp.bfloat16)

    def scaled_parts(ref, g, column, count):
        first = pl.multiple_of(g * GROUP, GROUP)
        weights = weight[pl.ds(first, GROUP), pl.ds(column, count)]
        return [
            (ref[first + i].astype(jnp.float32) * weights[i : i + 1, :]).astype(jnp.bfloat16)
            for i in range(GROUP)
        ]

    own_column = pl.multiple_of(s * width, width)

    def own_step(g, carry):
        squares, vector = carry
        parts = scaled_parts(jac, g, own_column, width)
        for i, part in enumerate(parts):
            wide = part.astype(jnp.float32)
            squares = squares + jnp.sum(
                (wide * wide).reshape(n_rows // 8, 8, width), axis=0
            )
            hit = jnp.dot(measured, part, preferred_element_type=jnp.float32)
            vector = vector + jnp.where(slot_col == g * GROUP + i, hit, 0.0)
        block = jnp.concatenate(parts, axis=0)
        own_t[:, pl.ds(pl.multiple_of(g * depth_rows, depth_rows), depth_rows)] = block.T
        return squares, vector

    squares, vector = lax.fori_loop(
        0,
        groups,
        own_step,
        (jnp.zeros((8, width), jnp.float32), jnp.zeros((n_slots, width), jnp.float32)),
    )
    rows = [factor[:, q * width : (q + 1) * width] for q in range(stripes)]
    rows.append(jnp.sum(squares, axis=0, keepdims=True))
    rows.append(jnp.sum(vector, axis=0, keepdims=True))
    rows.append(jnp.zeros((8 - len(rows), width), jnp.float32))
    small[t] = jnp.concatenate(rows, axis=0)

    def small_copy(source, target):
        return pltpu.make_async_remote_copy(
            src_ref=small.at[source],
            dst_ref=small.at[source],
            send_sem=small_send.at[target],
            recv_sem=small_recv.at[source],
            device_id=(target, s),
            device_id_type=MESH,
        )

    for step in range(1, n_tm):
        small_copy(t, lax.rem(t + step, n_tm)).start()

    def gram_chunk(ref, column):
        def body(g, total):
            block = jnp.concatenate(scaled_parts(ref, g, column, LANES), axis=0)
            rows = pl.ds(pl.multiple_of(g * depth_rows, depth_rows), depth_rows)
            return total + jnp.dot(own_t[:, rows], block, preferred_element_type=jnp.float32)

        return lax.fori_loop(0, groups, body, jnp.zeros((width, LANES), jnp.float32))

    def gram_copy(source, target):
        return pltpu.make_async_remote_copy(
            src_ref=outgoing.at[target],
            dst_ref=incoming.at[source],
            send_sem=gram_send.at[target],
            recv_sem=gram_recv.at[source],
            device_id=(target, s),
            device_id_type=MESH,
        )

    def send_chunk(gram, stripe, half):
        chunk = stripe * 2 + half
        decay = later[stripe, pl.ds(0, 1), lanes(half)]
        outgoing[chunk] = (gram * row_decay[...] * decay).astype(jnp.bfloat16)

        @pl.when(chunk != t)
        def _():
            gram_copy(t, chunk).start()

    own_grams = [
        gram_chunk(jac.at[:, :, lanes(half)], pl.multiple_of(s * width + half * LANES, LANES))
        for half in range(2)
    ]

    for step in range(1, n_tm):
        source = lax.rem(t + step, n_tm)
        small_copy(source, source).wait_recv()

    def own_row(values):
        mine = lax.broadcasted_iota(jnp.int32, (stripes, width), 0) == s
        return jnp.sum(jnp.where(mine, values, 0.0), axis=0, keepdims=True)

    product = jnp.ones((stripes, width), jnp.float32)
    diagonal = jnp.zeros((1, width), jnp.float32)
    info = jnp.zeros((1, width), jnp.float32)
    for block in range(n_tm):
        message = small[block]
        throughs = message[:stripes, :]
        product = jnp.where(block > t, product * throughs, product)
        through = own_row(throughs)
        more_diagonal = through * through * diagonal + message[stripes : stripes + 1, :]
        more_info = through * info + message[stripes + 1 : stripes + 2, :]
        diagonal = jnp.where(block <= t, more_diagonal, diagonal)
        info = jnp.where(block <= t, more_info, info)
    diag_out[...] = diagonal
    vec_out[...] = info
    for q in range(stripes):
        later[q] = jnp.broadcast_to(product[q : q + 1, :], (8, width))
    row_decay[...] = jnp.broadcast_to(own_row(product), (LANES, width)).T

    for half in range(2):
        send_chunk(own_grams[half], s, half)
    partner_copy.wait_recv()
    other = x * 2 + 1 - c
    for half in range(2):
        send_chunk(
            gram_chunk(
                partner_jac.at[:, :, lanes(half)],
                pl.multiple_of(other * width + half * LANES, LANES),
            ),
            other,
            half,
        )
    near = (1 - x) * 2 + c
    far = (1 - x) * 2 + 1 - c
    for phase in range(2):
        cross_copy(phase).wait_recv()
        relay_copy(phase).start()
        half = lax.rem(c + phase, 2)
        column = pl.multiple_of(near * width + half * LANES, LANES)
        send_chunk(gram_chunk(across_jac.at[phase], column), near, half)
        relay_copy(phase).wait_recv()
        half = lax.rem(1 - c + phase, 2)
        column = pl.multiple_of(far * width + half * LANES, LANES)
        send_chunk(gram_chunk(relay_jac.at[phase], column), far, half)

    total = outgoing[t].astype(jnp.float32)
    for step in range(1, n_tm):
        source = lax.rem(t + step, n_tm)
        gram_copy(source, source).wait_recv()
        total = total + incoming[source].astype(jnp.float32)
    info_out[...] = total

    for step in range(1, n_tm):
        target = lax.rem(t + step, n_tm)
        gram_copy(t, target).wait_send()
        small_copy(t, target).wait_send()
    partner_copy.wait_send()
    for phase in range(2):
        cross_copy(phase).wait_send()
        relay_copy(phase).wait_send()


def fused(n_tm, jacobian, measurement, depth_block, precision, valid_slot_counts, retention):
    n_slots, n_rows, width = jacobian.shape
    full = retention.shape[1]
    stripes = full // width
    vmem = pl.BlockSpec(memory_space=pltpu.VMEM)
    diagonal, vector, info = pl.pallas_call(
        functools.partial(filter_kernel, n_tm),
        out_shape=(
            jax.ShapeDtypeStruct((1, width), jnp.float32),
            jax.ShapeDtypeStruct((1, width), jnp.float32),
            jax.ShapeDtypeStruct((width, LANES), jnp.float32),
        ),
        in_specs=[vmem] * 4 + [pl.BlockSpec(memory_space=pltpu.SMEM), vmem],
        out_specs=(vmem, vmem, vmem),
        scratch_shapes=[
            pltpu.VMEM((n_slots, n_rows, width), jnp.bfloat16),
            pltpu.VMEM((2, n_slots, n_rows, LANES), jnp.bfloat16),
            pltpu.VMEM((2, n_slots, n_rows, LANES), jnp.bfloat16),
            pltpu.VMEM((n_slots, full), jnp.float32),
            pltpu.VMEM((width, n_slots * n_rows), jnp.bfloat16),
            pltpu.VMEM((n_tm, 8, width), jnp.float32),
            pltpu.VMEM((stripes, 8, width), jnp.float32),
            pltpu.VMEM((width, LANES), jnp.float32),
            pltpu.VMEM((n_tm, width, LANES), jnp.bfloat16),
            pltpu.VMEM((n_tm, width, LANES), jnp.bfloat16),
            pltpu.SemaphoreType.DMA((5,)),
            pltpu.SemaphoreType.DMA((5,)),
            pltpu.SemaphoreType.DMA((n_tm,)),
            pltpu.SemaphoreType.DMA((n_tm,)),
            pltpu.SemaphoreType.DMA((n_tm,)),
            pltpu.SemaphoreType.DMA((n_tm,)),
        ],
        compiler_params=pltpu.CompilerParams(collective_id=0, has_side_effects=True),
    )(
        jacobian,
        measurement,
        depth_block[None, :],
        precision[None, :],
        valid_slot_counts,
        retention,
    )
    return diagonal.reshape(width), vector.reshape(width), info


def solution(mesh):
    n_tm, stripes = mesh.shape["tm"], mesh.shape["state"]

    def body(jacobian, measurement, depth_block, precision, valid_slot_counts, retention):
        args = (jacobian, measurement, depth_block, precision, valid_slot_counts, retention)
        n_slots, _, width = jacobian.shape
        if stripes == 4 and width == 2 * LANES and n_tm * LANES == width * stripes and n_slots % GROUP == 0:
            return fused(n_tm, *args)
        return local(*args)

    in_specs = (P("tm", None, "state"), P("tm", None), P("tm"), P(), P("tm"), P("tm", None))
    out_specs = (P(("tm", "state")), P(("tm", "state")), P("state", "tm"))
    return jax.shard_map(body, mesh=mesh, in_specs=in_specs, out_specs=out_specs, check_vma=False)
```
